256 devices in a mesh: snap: 4 (over y_hi, core), slab: 64 (over z, x, y_lo).
Axes of the slice: x: 4, y: 4 (y_hi: 2, y_lo: 2; y = y_hi * 2 + y_lo), z: 8, core: 2. Of those that a mesh axis runs over, the one named last changes fastest.
Arguments:
- velocity: bfloat16 [64, 3, 512, 16, 512], P('snap', None, 'slab'), may hold values from -6 to 6
- phase_bins: int32 [64], P('snap'), may hold values from 0 to 179, as said below
Outputs:
- coefficients: float32 [3, 3, 4, 512, 16, 512], P(None, None, None, 'slab', None, 'snap')
The draws below stay inside these ranges and needn't reach their ends.
Inputs may be any that keep to these rules, and one draw needn't show every extreme that they name: `phase_bins`: no two snapshots share a bin, and the bins of all snapshots spread over the whole revolution.
All inputs are finite; a program needn't handle non-finite values.
Results may differ from the reference program's by a relative error of at most 0.0003.
Values may be sent and summed in bfloat16 or wider, within the bound.
A program may use at most 128 MiB of HBM per device.

```python
import jax
import jax.numpy as jnp
from jax import lax

NY = 16
NZ = 512
BINS = 180
BASIS = 3
ORDERS = 4
NSNAP = 64
NX = 512


def draw_phase_bins(key, part):
    first_key = jax.random.fold_in(key, 11)
    second_key = jax.random.fold_in(key, 23)
    strata = jax.random.permutation(first_key, jnp.arange(NSNAP, dtype=jnp.int32))
    jitter = jax.random.randint(second_key, (NSNAP,), 0, max(BINS // NSNAP, 1), dtype=jnp.int32)
    return (strata * BINS // NSNAP + jitter).astype(jnp.int32)


def block_levels(rng, dims, pieces, smallest, top_value):
    factor_of = 1.0
    for dim, shards_of in pieces:
        steps = jax.random.uniform(jax.random.fold_in(jax.random.fold_in(rng, 6), dim), (shards_of,), jnp.float32, smallest / len(pieces), top_value / len(pieces))
        factor_of = factor_of * jnp.repeat(jnp.exp(steps), dims[dim] // shards_of).reshape((-1,) + (1,) * (len(dims) - 1 - dim))
    return factor_of


def normal_values(key, shape, width, bound, split=(), kind=jnp.bfloat16):
    loudness = block_levels(key, shape, split, -0.22, 0.18) if split else 1.0
    drawn = jax.random.normal(key, shape, jnp.float32) * width * loudness
    return jnp.minimum(jnp.maximum(drawn, -bound), bound).astype(kind)


def setup_inputs(seed: int = 0) -> dict:
    streams_of = jax.random.split(jax.random.key(seed), 3)
    velocity = normal_values(streams_of[0], (NSNAP, 3, NX, NY, NZ), 1.0, 6.0, ((0, 4), (2, 64)))
    phase_bins = draw_phase_bins(jax.random.fold_in(streams_of[2], 71), 0)
    return {"velocity": velocity, "phase_bins": phase_bins}


inv_spacing = 0.75


def central(padded, direction):
    extent = padded.shape[-3:]
    leading = [slice(None)] * (padded.ndim - 3)

    def shifted(offset):
        window = [slice(2, extent[0] - 2), slice(2, extent[1] - 2), slice(2, extent[2] - 2)]
        window[direction] = slice(offset, extent[direction] - 4 + offset)
        return padded[tuple(leading + window)].astype(jnp.float32)

    return (8.0 * (shifted(3) - shifted(1)) - (shifted(4) - shifted(0))) * (inv_spacing / 12.0)


def vorticity_of(comp_u, comp_v, comp_w):
    omega_x = central(comp_w, 1) - central(comp_v, 2)
    omega_y = central(comp_u, 2) - central(comp_w, 0)
    omega_z = central(comp_v, 0) - central(comp_u, 1)
    return jnp.stack([omega_x, omega_y, omega_z], axis=-4)


def basis_weights(phase_bins):
    centers = (jnp.arange(BINS, dtype=jnp.float32) + 0.5) * (2.0 * jnp.pi / BINS)
    table = jnp.stack([jnp.ones_like(centers), jnp.cos(centers), jnp.sin(centers)], axis=1)
    onehot = (phase_bins[:, None] == jnp.arange(BINS, dtype=jnp.int32)[None, :]).astype(jnp.float32)
    return jnp.dot(onehot, table, precision=lax.Precision.HIGHEST)


def invert_three(gram):
    g00, g01, g02 = gram[0, 0], gram[0, 1], gram[0, 2]
    g10, g11, g12 = gram[1, 0], gram[1, 1], gram[1, 2]
    g20, g21, g22 = gram[2, 0], gram[2, 1], gram[2, 2]
    c00 = g11 * g22 - g12 * g21
    c01 = g02 * g21 - g01 * g22
    c02 = g01 * g12 - g02 * g11
    c10 = g12 * g20 - g10 * g22
    c11 = g00 * g22 - g02 * g20
    c12 = g02 * g10 - g00 * g12
    c20 = g10 * g21 - g11 * g20
    c21 = g01 * g20 - g00 * g21
    c22 = g00 * g11 - g01 * g10
    determinant = g00 * c00 + g01 * c10 + g02 * c20
    adjugate = jnp.stack([jnp.stack([c00, c01, c02]), jnp.stack([c10, c11, c12]), jnp.stack([c20, c21, c22])])
    return adjugate / determinant


def reference(velocity, phase_bins):
    weights = basis_weights(phase_bins)

    def accumulate(total, inputs):
        snapshot_field, weight_row = inputs
        padded = jnp.pad(snapshot_field.astype(jnp.float32), ((0, 0), (2, 2), (2, 2), (2, 2)))
        omega = vorticity_of(padded[0], padded[1], padded[2])
        squared = omega * omega
        powers = jnp.stack([omega, squared, squared * omega, squared * squared], axis=1)
        return total + weight_row[:, None, None, None, None, None] * powers[None], None

    start = jnp.zeros((BASIS, 3, ORDERS, NX, NY, NZ), jnp.float32)
    sums, _ = lax.scan(accumulate, start, (velocity, weights))
    gram = jnp.dot(weights.T, weights, precision=lax.Precision.HIGHEST)
    inverse = invert_three(gram)
    return jnp.einsum('ij,j...->i...', inverse, sums, precision=lax.Precision.HIGHEST)
```

```python
import functools

import jax
import jax.numpy as jnp
import numpy as np
from jax import lax
from jax.experimental import pallas as pl
from jax.experimental.pallas import tpu as pltpu
from jax.sharding import PartitionSpec as P

MESH = pl.DeviceIdType.MESH
BINS = 180
NEAR = 0.75 * 8.0 / 12.0
WIDE = 0.75 / 12.0
PLANES = ((2, 3, 4, 5), (0, 1, 6, 7))
NS, NP, NY, NZ = 16, 8, 16, 512
LANES = 128


def band(n):
    d = np.zeros((n, n), np.float32)
    for i in range(n):
        for o, c in ((1, NEAR), (-1, -NEAR), (2, -WIDE), (-2, WIDE)):
            if 0 <= i + o < n:
                d[i, i + o] = c
    return d


def stencils():
    along_y = np.kron(np.eye(NP, dtype=np.float32), band(NY))
    along_x = np.kron(band(NP + 4), np.eye(NY, dtype=np.float32))
    left_w, left_vu, left_halo = [], [], []
    for planes in PLANES:
        rows = np.concatenate([np.arange(p * NY, (p + 1) * NY) for p in planes])
        dy = along_y[rows]
        dx_ext = along_x[rows + 2 * NY]
        dx = dx_ext[:, 2 * NY : 2 * NY + NP * NY]
        halo = np.concatenate([dx_ext[:, : 2 * NY], dx_ext[:, -2 * NY :]], axis=1)
        left_w.append(np.concatenate([dy, -dx], axis=0))
        left_vu.append(np.concatenate([dx, -dy], axis=1))
        left_halo.append(halo)
    return [
        np.stack(left_w),
        np.stack(left_vu),
        left_halo[1],
        band(NZ).T.copy(),
    ]


def dot(a, b):
    return jnp.dot(a, b, preferred_element_type=jnp.float32)


def kernel(
    vel_hbm, bins, left_w, left_vu, left_halo, right_z, out,
    vel, halo, omega, weights, sums, mate, cross_out, cross_in, gram_out, gram_in,
    load_sem, halo_send, halo_recv, mate_send, mate_recv, cross_send, cross_recv, gram_send, gram_recv,
):
    snap, slab = lax.axis_index("snap"), lax.axis_index("slab")
    slabs = lax.axis_size("slab")
    core, chip = snap % 2, snap // 2
    has_lo, has_hi = slab > 0, slab < slabs - 1
    lo_peer = (snap, jnp.maximum(slab - 1, 0))
    hi_peer = (snap, jnp.minimum(slab + 1, slabs - 1))
    mate_peer = (chip * 2 + 1 - core, slab)
    cross_peer = ((1 - chip) * 2 + core, slab)
    snap_peers = [((snap + d) % 4, slab) for d in (1, 2, 3)]

    def zone(i):
        side = (chip + 1 - i // 2) % 2
        return pl.ds(pl.multiple_of((side * 2 + (core + 1 + i) % 2) * LANES, LANES), LANES)

    load = pltpu.make_async_copy(vel_hbm, vel, load_sem)
    load.start()

    barrier = pltpu.get_barrier_semaphore()
    for peer in snap_peers:
        pl.semaphore_signal(barrier, inc=1, device_id=peer, device_id_type=MESH)
    for cond, peer in ((has_lo, lo_peer), (has_hi, hi_peer)):
        @pl.when(cond)
        def _(peer=peer):
            pl.semaphore_signal(barrier, inc=1, device_id=peer, device_id_type=MESH)
    pl.semaphore_wait(barrier, 3 + has_lo.astype(jnp.int32) + has_hi.astype(jnp.int32))

    def halo_copy(i, side):
        planes = pl.ds(NP - 2, 2) if side == 0 else pl.ds(0, 2)
        return pltpu.make_async_remote_copy(
            src_ref=vel_hbm.at[:, pl.ds(1, 2), planes, :, zone(i)],
            dst_ref=halo.at[i, :, :, side],
            send_sem=halo_send.at[i, side],
            recv_sem=halo_recv.at[i, side],
            device_id=hi_peer if side == 0 else lo_peer,
            device_id_type=MESH,
        )

    for i in range(4):
        for side, cond in ((0, has_hi), (1, has_lo)):
            @pl.when(cond)
            def _(i=i, side=side):
                halo_copy(i, side).start()

    for side, cond in ((0, has_lo), (1, has_hi)):
        @pl.when(jnp.logical_not(cond))
        def _(side=side):
            for i in range(4):
                halo[i, :, :, side] = jnp.zeros((NS, 2, 2, NY, LANES), jnp.bfloat16)

    zero = jnp.zeros((8, LANES), jnp.float32)

    def weigh(s, g):
        angle = (jnp.full((8, LANES), bins[s], jnp.int32).astype(jnp.float32) + 0.5) * (
            2.0 * np.pi / BINS
        )
        c, n = jnp.cos(angle), jnp.sin(angle)
        weights[0, s] = c
        weights[1, s] = n
        return (g[0] + c, g[1] + n, g[2] + c * c, g[3] + c * n, g[4] + n * n)

    for n, value in enumerate(lax.fori_loop(0, NS, weigh, (zero,) * 5)):
        gram_out[n] = value

    def gram_copy(d):
        return pltpu.make_async_remote_copy(
            src_ref=gram_out, dst_ref=gram_in.at[d],
            send_sem=gram_send.at[d], recv_sem=gram_recv.at[d],
            device_id=snap_peers[d], device_id_type=MESH,
        )

    load.wait()

    def derive(i, p):
        z = zone(i)
        planes = PLANES[p]

        def own(s, comp):
            if p == 0:
                return vel[s, comp, 2:6].reshape(64, NZ)
            return jnp.concatenate([vel[s, comp, 0:2], vel[s, comp, 6:8]], axis=0).reshape(64, NZ)

        def body(s, carry):
            uv = jnp.concatenate([own(s, 0), own(s, 1)], axis=0)
            dz = dot(uv, right_z[:, z])
            v_u = jnp.concatenate(
                [vel[s, 1, :, :, z].reshape(NP * NY, LANES), vel[s, 0, :, :, z].reshape(NP * NY, LANES)],
                axis=0,
            )
            w = vel[s, 2, :, :, z].reshape(NP * NY, LANES)
            from_w = dot(left_w[p], w)
            om_z = dot(left_vu[p], v_u)
            om_x = from_w[:64] - dz[64:]
            om_y = from_w[64:] + dz[:64]
            if p == 1:
                v_halo = halo[i, s, 0].reshape(64, LANES)
                w_halo = halo[i, s, 1].reshape(64, LANES)
                om_z = om_z + dot(left_halo[...], v_halo)
                om_y = om_y - dot(left_halo[...], w_halo)
            omega[s, 0] = om_x.reshape(8, 8, LANES)
            omega[s, 1] = om_y.reshape(8, 8, LANES)
            omega[s, 2] = om_z.reshape(8, 8, LANES)
            return carry

        lax.fori_loop(0, NS, body, 0)

    def accumulate(i, p):
        def body(t, carry):
            c, r = t // 4, t % 4
            rows = pl.ds(2 * r, 2)
            acc = [[None] * 4 for _ in range(3)]
            for s in range(NS):
                om = omega[s, c, rows]
                sq = om * om
                powers = (om, sq, sq * om, sq * sq)
                for k in range(4):
                    for j in range(3):
                        term = powers[k] if j == 0 else weights[j - 1, s][None] * powers[k]
                        acc[j][k] = term if s == 0 else acc[j][k] + term
            for j in range(3):
                for k in range(4):
                    sums[i, p, j, c * 4 + k, rows] = acc[j][k]
            return carry

        lax.fori_loop(0, 12, body, 0)

    def mate_copy(half, p):
        return pltpu.make_async_remote_copy(
            src_ref=sums.at[2 * half, p], dst_ref=mate.at[half, p],
            send_sem=mate_send.at[half, p], recv_sem=mate_recv.at[half, p],
            device_id=mate_peer, device_id_type=MESH,
        )

    def cross_copy(p):
        return pltpu.make_async_remote_copy(
            src_ref=cross_out.at[p], dst_ref=cross_in.at[p],
            send_sem=cross_send.at[p], recv_sem=cross_recv.at[p],
            device_id=cross_peer, device_id_type=MESH,
        )

    for p in range(2):
        for i in range(4):
            if p == 1:
                for side, cond, gone in ((0, has_lo, has_hi), (1, has_hi, has_lo)):
                    @pl.when(cond)
                    def _(i=i, side=side):
                        halo_copy(i, side).wait_recv()
            derive(i, p)
            accumulate(i, p)
            if p == 0 and i == 0:
                for d in range(3):
                    gram_copy(d).start()
            if i % 2 == 0:
                mate_copy(i // 2, p).start()
            if i == 1:
                mate_copy(0, p).wait_recv()

                def add(t, carry, p=p):
                    for j in range(3):
                        cross_out[p, j, t] = sums[1, p, j, t] + mate[0, p, j, t]
                    return carry

                lax.fori_loop(0, 12, add, 0)
                cross_copy(p).start()

    for d in range(3):
        gram_copy(d).wait()
    g = [gram_out[n] + gram_in[0, n] + gram_in[1, n] + gram_in[2, n] for n in range(5)]
    g00 = jnp.full((8, LANES), 4.0 * NS, jnp.float32)
    g01, g02, g11, g12, g22 = g
    c00 = g11 * g22 - g12 * g12
    c01 = g02 * g12 - g01 * g22
    c02 = g01 * g12 - g02 * g11
    c11 = g00 * g22 - g02 * g02
    c12 = g02 * g01 - g00 * g12
    c22 = g00 * g11 - g01 * g01
    det = g00 * c00 + g01 * c01 + g02 * c02
    inverse = [[x / det for x in row] for row in ((c00, c01, c02), (c01, c11, c12), (c02, c12, c22))]

    for p in range(2):
        mate_copy(1, p).wait_recv()
        cross_copy(p).wait_recv()

        def solve(t, carry, p=p):
            total = [sums[3, p, j, t] + mate[1, p, j, t] + cross_in[p, j, t] for j in range(3)]
            for n in range(3):
                fit = sum(inverse[n][j][None] * total[j] for j in range(3)).reshape(4, NY, LANES)
                if p == 0:
                    out[n, t // 4, t % 4, 2:6] = fit
                else:
                    out[n, t // 4, t % 4, 0:2] = fit[:2]
                    out[n, t // 4, t % 4, 6:8] = fit[2:]
            return carry

        lax.fori_loop(0, 12, solve, 0)

    for i in range(4):
        for side, cond in ((0, has_hi), (1, has_lo)):
            @pl.when(cond)
            def _(i=i, side=side):
                halo_copy(i, side).wait_send()
    for p in range(2):
        cross_copy(p).wait_send()
        for half in range(2):
            mate_copy(half, p).wait_send()


def local(velocity, phase_bins):
    consts = [jnp.asarray(m, jnp.bfloat16) for m in stencils()]
    vmem = pl.BlockSpec(memory_space=pltpu.VMEM)
    f32, bf16, dma = jnp.float32, jnp.bfloat16, pltpu.SemaphoreType.DMA
    block = (3, 12, 8, 8, LANES)
    return pl.pallas_call(
        kernel,
        out_shape=jax.ShapeDtypeStruct((3, 3, 4, NP, NY, LANES), f32),
        in_specs=[pl.BlockSpec(memory_space=pl.ANY), pl.BlockSpec(memory_space=pltpu.SMEM)] + [vmem] * 4,
        out_specs=vmem,
        scratch_shapes=[
            pltpu.VMEM((NS, 3, NP, NY, NZ), bf16),
            pltpu.VMEM((4, NS, 2, 2, 2, NY, LANES), bf16),
            pltpu.VMEM((NS, 3, 8, 8, LANES), f32),
            pltpu.VMEM((2, NS, 8, LANES), f32),
            pltpu.VMEM((4, 2) + block, f32),
            pltpu.VMEM((2, 2) + block, f32),
            pltpu.VMEM((2,) + block, f32),
            pltpu.VMEM((2,) + block, f32),
            pltpu.VMEM((5, 8, LANES), f32),
            pltpu.VMEM((3, 5, 8, LANES), f32),
            dma, dma((4, 2)), dma((4, 2)), dma((2, 2)), dma((2, 2)), dma((2,)), dma((2,)), dma((3,)), dma((3,)),
        ],
        compiler_params=pltpu.CompilerParams(collective_id=0, has_side_effects=True),
    )(velocity, phase_bins, *consts)


def solution(mesh):
    in_specs = (P("snap", None, "slab", None, None), P("snap"))
    out_specs = P(None, None, None, "slab", None, "snap")
    return jax.shard_map(local, mesh=mesh, in_specs=in_specs, out_specs=out_specs, check_vma=False)
```

```python
import functools

import jax
import jax.numpy as jnp
import numpy as np
from jax import lax
from jax.experimental import pallas as pl
from jax.experimental.pallas import tpu as pltpu
from jax.sharding import PartitionSpec as P

MESH = pl.DeviceIdType.MESH
BINS = 180
NEAR = 0.75 * 8.0 / 12.0
WIDE = 0.75 / 12.0
PLANES = ((2, 3, 4, 5), (0, 1, 6, 7))
NS, NP, NY, NZ = 16, 8, 16, 512
LANES = 128
TOP = 32766.0


def band(n):
    d = np.zeros((n, n), np.float32)
    for i in range(n):
        for o, c in ((1, NEAR), (-1, -NEAR), (2, -WIDE), (-2, WIDE)):
            if 0 <= i + o < n:
                d[i, i + o] = c
    return d


def stencils():
    along_y = np.kron(np.eye(NP, dtype=np.float32), band(NY))
    along_x = np.kron(band(NP + 4), np.eye(NY, dtype=np.float32))
    left_w, left_vu, left_halo = [], [], []
    for planes in PLANES:
        rows = np.concatenate([np.arange(p * NY, (p + 1) * NY) for p in planes])
        dy = along_y[rows]
        dx_ext = along_x[rows + 2 * NY]
        dx = dx_ext[:, 2 * NY : 2 * NY + NP * NY]
        halo = np.concatenate([dx_ext[:, : 2 * NY], dx_ext[:, -2 * NY :]], axis=1)
        left_w.append(np.concatenate([dy, -dx], axis=0))
        left_vu.append(np.concatenate([dx, -dy], axis=1))
        left_halo.append(halo)
    return [
        np.stack(left_w),
        np.stack(left_vu),
        left_halo[1],
        band(NZ).T.copy(),
    ]


def dot(a, b):
    return jnp.dot(a, b, preferred_element_type=jnp.float32)


def kernel(
    vel_hbm, bins, *refs):
    consts_hbm, out, consts, refs = refs[:4], refs[4], refs[5:9], refs[9:]
    left_w, left_vu, left_halo, right_z = consts
    (vel, halo, omega, weights, sums, mate, cross_out, cross_in, step_out, step_in, gram_out, gram_in,
    load_sem, halo_send, halo_recv, mate_send, mate_recv, cross_send, cross_recv, step_send, step_recv, gram_send, gram_recv, const_sem) = refs
    snap, slab = lax.axis_index("snap"), lax.axis_index("slab")
    slabs = lax.axis_size("slab")
    core, chip = snap % 2, snap // 2
    has_lo, has_hi = slab > 0, slab < slabs - 1
    lo_peer = (snap, jnp.maximum(slab - 1, 0))
    hi_peer = (snap, jnp.minimum(slab + 1, slabs - 1))
    mate_peer = (chip * 2 + 1 - core, slab)
    cross_peer = ((1 - chip) * 2 + core, slab)
    snap_peers = [((snap + d) % 4, slab) for d in (1, 2, 3)]

    def zone(i):
        side = (chip + 1 - i // 2) % 2
        return pl.ds(pl.multiple_of((side * 2 + (core + 1 + i) % 2) * LANES, LANES), LANES)

    load = pltpu.make_async_copy(vel_hbm, vel, load_sem)
    load.start()
    const_loads = [
        pltpu.make_async_copy(consts_hbm[n], consts[n], const_sem.at[n]) for n in range(4)
    ]
    for const_load in const_loads:
        const_load.start()

    barrier = pltpu.get_barrier_semaphore()
    for peer in snap_peers:
        pl.semaphore_signal(barrier, inc=1, device_id=peer, device_id_type=MESH)
    for cond, peer in ((has_lo, lo_peer), (has_hi, hi_peer)):
        @pl.when(cond)
        def _(peer=peer):
            pl.semaphore_signal(barrier, inc=1, device_id=peer, device_id_type=MESH)
    pl.semaphore_wait(barrier, 3 + has_lo.astype(jnp.int32) + has_hi.astype(jnp.int32))

    def halo_copy(i, side):
        planes = pl.ds(NP - 2, 2) if side == 0 else pl.ds(0, 2)
        return pltpu.make_async_remote_copy(
            src_ref=vel_hbm.at[:, pl.ds(1, 2), planes, :, zone(i)],
            dst_ref=halo.at[i, :, :, side],
            send_sem=halo_send.at[i, side],
            recv_sem=halo_recv.at[i, side],
            device_id=hi_peer if side == 0 else lo_peer,
            device_id_type=MESH,
        )

    for i in range(4):
        for side, cond in ((0, has_hi), (1, has_lo)):
            @pl.when(cond)
            def _(i=i, side=side):
                halo_copy(i, side).start()

    for side, cond in ((0, has_lo), (1, has_hi)):
        @pl.when(jnp.logical_not(cond))
        def _(side=side):
            for i in range(4):
                halo[i, :, :, side] = jnp.zeros((NS, 2, 2, NY, LANES), jnp.bfloat16)

    zero = jnp.zeros((8, LANES), jnp.float32)

    def weigh(s, g):
        angle = (jnp.full((8, LANES), bins[s], jnp.int32).astype(jnp.float32) + 0.5) * (
            2.0 * np.pi / BINS
        )
        c, n = jnp.cos(angle), jnp.sin(angle)
        weights[0, s] = c
        weights[1, s] = n
        return (g[0] + c, g[1] + n, g[2] + c * c, g[3] + c * n, g[4] + n * n)

    for n, value in enumerate(lax.fori_loop(0, NS, weigh, (zero,) * 5)):
        gram_out[n] = value

    def gram_copy(d):
        return pltpu.make_async_remote_copy(
            src_ref=gram_out, dst_ref=gram_in.at[d],
            send_sem=gram_send.at[d], recv_sem=gram_recv.at[d],
            device_id=snap_peers[d], device_id_type=MESH,
        )

    load.wait()
    for const_load in const_loads:
        const_load.wait()

    def derive(i, p):
        z = zone(i)
        planes = PLANES[p]

        def own(s, comp):
            if p == 0:
                return vel[s, comp, 2:6].reshape(64, NZ)
            return jnp.concatenate([vel[s, comp, 0:2], vel[s, comp, 6:8]], axis=0).reshape(64, NZ)

        def body(s, carry):
            uv = jnp.concatenate([own(s, 0), own(s, 1)], axis=0)
            dz = dot(uv, right_z[:, z])
            v_u = jnp.concatenate(
                [vel[s, 1, :, :, z].reshape(NP * NY, LANES), vel[s, 0, :, :, z].reshape(NP * NY, LANES)],
                axis=0,
            )
            w = vel[s, 2, :, :, z].reshape(NP * NY, LANES)
            from_w = dot(left_w[p], w)
            om_z = dot(left_vu[p], v_u)
            om_x = from_w[:64] - dz[64:]
            om_y = from_w[64:] + dz[:64]
            if p == 1:
                v_halo = halo[i, s, 0].reshape(64, LANES)
                w_halo = halo[i, s, 1].reshape(64, LANES)
                om_z = om_z + dot(left_halo[...], v_halo)
                om_y = om_y - dot(left_halo[...], w_halo)
            omega[s, 0] = om_x.reshape(8, 8, LANES)
            omega[s, 1] = om_y.reshape(8, 8, LANES)
            omega[s, 2] = om_z.reshape(8, 8, LANES)
            return carry

        lax.fori_loop(0, NS, body, 0)

    def accumulate(i, p):
        def body(t, carry):
            c, r = t // 4, t % 4
            rows = pl.ds(2 * r, 2)
            acc = [[None] * 4 for _ in range(3)]
            for s in range(NS):
                om = omega[s, c, rows]
                sq = om * om
                powers = (om, sq, sq * om, sq * sq)
                for k in range(4):
                    for j in range(3):
                        term = powers[k] if j == 0 else weights[j - 1, s][None] * powers[k]
                        acc[j][k] = term if s == 0 else acc[j][k] + term
            for j in range(3):
                for k in range(4):
                    sums[i, p, j, c * 4 + k, rows] = acc[j][k]
            return carry

        lax.fori_loop(0, 12, body, 0)

    def mate_copy(half, p):
        return pltpu.make_async_remote_copy(
            src_ref=sums.at[2 * half, p], dst_ref=mate.at[half, p],
            send_sem=mate_send.at[half, p], recv_sem=mate_recv.at[half, p],
            device_id=mate_peer, device_id_type=MESH,
        )

    def cross_copy(p):
        return pltpu.make_async_remote_copy(
            src_ref=cross_out.at[p], dst_ref=cross_in.at[p],
            send_sem=cross_send.at[p], recv_sem=cross_recv.at[p],
            device_id=cross_peer, device_id_type=MESH,
        )

    def step_copy(p):
        return pltpu.make_async_remote_copy(
            src_ref=step_out.at[p], dst_ref=step_in.at[p],
            send_sem=step_send.at[p], recv_sem=step_recv.at[p],
            device_id=cross_peer, device_id_type=MESH,
        )

    for p in range(2):
        for i in range(4):
            if p == 1:
                for side, cond, gone in ((0, has_lo, has_hi), (1, has_hi, has_lo)):
                    @pl.when(cond)
                    def _(i=i, side=side):
                        halo_copy(i, side).wait_recv()
            derive(i, p)
            accumulate(i, p)
            if p == 0 and i == 0:
                for d in range(3):
                    gram_copy(d).start()
            if i % 2 == 0:
                mate_copy(i // 2, p).start()
            if i == 1:
                mate_copy(0, p).wait_recv()

                def add(t, carry, p=p):
                    for j in range(3):
                        total = sums[1, p, j, t] + mate[0, p, j, t]
                        top = jnp.maximum(jnp.max(jnp.abs(total), axis=(0, 1))[None], 1e-33)
                        code = jnp.round(total * (TOP / top)[None]).astype(jnp.int32)
                        cross_out[p, j, t] = code.astype(jnp.int16).reshape(4, NY, LANES)
                        step_out[p, j, pl.ds(t, 1)] = top * (1.0 / TOP)
                    return carry

                lax.fori_loop(0, 12, add, 0)
                step_copy(p).start()
                cross_copy(p).start()

    for d in range(3):
        gram_copy(d).wait()
    g = [gram_out[n] + gram_in[0, n] + gram_in[1, n] + gram_in[2, n] for n in range(5)]
    g00 = jnp.full((8, LANES), 4.0 * NS, jnp.float32)
    g01, g02, g11, g12, g22 = g
    c00 = g11 * g22 - g12 * g12
    c01 = g02 * g12 - g01 * g22
    c02 = g01 * g12 - g02 * g11
    c11 = g00 * g22 - g02 * g02
    c12 = g02 * g01 - g00 * g12
    c22 = g00 * g11 - g01 * g01
    det = g00 * c00 + g01 * c01 + g02 * c02
    inverse = [[x / det for x in row] for row in ((c00, c01, c02), (c01, c11, c12), (c02, c12, c22))]

    for p in range(2):
        mate_copy(1, p).wait_recv()
        step_copy(p).wait_recv()
        cross_copy(p).wait_recv()

        def solve(t, carry, p=p):
            total = [
                sums[3, p, j, t]
                + mate[1, p, j, t]
                + cross_in[p, j, t].astype(jnp.int32).astype(jnp.float32).reshape(8, 8, LANES)
                * step_in[p, j, pl.ds(t, 1)][None]
                for j in range(3)
            ]
            for n in range(3):
                fit = sum(inverse[n][j][None] * total[j] for j in range(3)).reshape(4, NY, LANES)
                if p == 0:
                    out[n, t // 4, t % 4, 2:6] = fit
                else:
                    out[n, t // 4, t % 4, 0:2] = fit[:2]
                    out[n, t // 4, t % 4, 6:8] = fit[2:]
            return carry

        lax.fori_loop(0, 12, solve, 0)

    for i in range(4):
        for side, cond in ((0, has_hi), (1, has_lo)):
            @pl.when(cond)
            def _(i=i, side=side):
                halo_copy(i, side).wait_send()
    for p in range(2):
        cross_copy(p).wait_send()
        step_copy(p).wait_send()
        for half in range(2):
            mate_copy(half, p).wait_send()


def local(velocity, phase_bins):
    consts = [jnp.asarray(m, jnp.bfloat16) for m in stencils()]
    hbm = pl.BlockSpec(memory_space=pl.ANY)
    f32, bf16, dma = jnp.float32, jnp.bfloat16, pltpu.SemaphoreType.DMA
    block = (3, 12, 8, 8, LANES)
    return pl.pallas_call(
        kernel,
        out_shape=jax.ShapeDtypeStruct((3, 3, 4, NP, NY, LANES), f32),
        in_specs=[hbm, pl.BlockSpec(memory_space=pltpu.SMEM)] + [hbm] * 4,
        out_specs=pl.BlockSpec(memory_space=pltpu.VMEM),
        scratch_shapes=[pltpu.VMEM(c.shape, bf16) for c in consts]
        + [
            pltpu.VMEM((NS, 3, NP, NY, NZ), bf16),
            pltpu.VMEM((4, NS, 2, 2, 2, NY, LANES), bf16),
            pltpu.VMEM((NS, 3, 8, 8, LANES), f32),
            pltpu.VMEM((2, NS, 8, LANES), f32),
            pltpu.VMEM((4, 2) + block, f32),
            pltpu.VMEM((2, 2) + block, f32),
            pltpu.VMEM((2, 3, 12, 4, NY, LANES), jnp.int16),
            pltpu.VMEM((2, 3, 12, 4, NY, LANES), jnp.int16),
            pltpu.VMEM((2, 3, 16, LANES), f32),
            pltpu.VMEM((2, 3, 16, LANES), f32),
            pltpu.VMEM((5, 8, LANES), f32),
            pltpu.VMEM((3, 5, 8, LANES), f32),
            dma, dma((4, 2)), dma((4, 2)), dma((2, 2)), dma((2, 2)), dma((2,)), dma((2,)), dma((2,)), dma((2,)), dma((3,)), dma((3,)), dma((4,)),
        ],
        compiler_params=pltpu.CompilerParams(collective_id=0, has_side_effects=True),
    )(velocity, phase_bins, *consts)


def solution(mesh):
    in_specs = (P("snap", None, "slab", None, None), P("snap"))
    out_specs = P(None, None, None, "slab", None, "snap")
    return jax.shard_map(local, mesh=mesh, in_specs=in_specs, out_specs=out_specs, check_vma=False)
```

```python
import functools

import jax
import jax.numpy as jnp
import numpy as np
from jax import lax
from jax.experimental import pallas as pl
from jax.experimental.pallas import tpu as pltpu
from jax.sharding import PartitionSpec as P

MESH = pl.DeviceIdType.MESH
BINS = 180
NEAR = 0.75 * 8.0 / 12.0
WIDE = 0.75 / 12.0
PLANES = ((2, 3, 4, 5), (0, 1, 6, 7))
NS, NP, NY, NZ = 16, 8, 16, 512
LANES = 128
TOP = 32766.0


def band(d):
    near = jnp.where(d == 1, NEAR, jnp.where(d == -1, -NEAR, 0.0))
    return near + jnp.where(d == 2, -WIDE, jnp.where(d == -2, WIDE, 0.0))


def grid(rows, cols):
    return [lax.broadcasted_iota(jnp.int32, (rows, cols), n) for n in (0, 1)]


def fill_stencils(left_w, left_vu, left_halo, right_z):
    bf16 = jnp.bfloat16
    for p in range(2):
        r, c = grid(64, NP * NY)
        plane = (r >> 4) + (2 if p == 0 else (r >> 5) * 4)
        same_y, same_x = (r & 15) == (c & 15), plane == (c >> 4)
        dx = jnp.where(same_y, band((c >> 4) - plane), 0.0)
        dy = jnp.where(same_x, band((c & 15) - (r & 15)), 0.0)
        left_w[p, 0:64] = dy.astype(bf16)
        left_w[p, 64:128] = (-dx).astype(bf16)
        left_vu[p, :, 0:128] = dx.astype(bf16)
        left_vu[p, :, 128:256] = (-dy).astype(bf16)
    r, c = grid(64, 64)
    plane = (r >> 4) + (r >> 5) * 4
    beyond = (c >> 4) - 2 + (c >> 5) * 8
    left_halo[...] = jnp.where((r & 15) == (c & 15), band(beyond - plane), 0.0).astype(bf16)
    r, c = grid(NZ, NZ)
    right_z[...] = band(r - c).astype(bf16)


def dot(a, b):
    return jnp.dot(a, b, preferred_element_type=jnp.float32)


def kernel(
    vel_hbm, bins_hbm, out, *refs):
    consts, refs = refs[:4], refs[4:]
    left_w, left_vu, left_halo, right_z = consts
    (bins, vel, halo, omega, weights, sums, mate, cross_out, cross_in, steps, step_out, step_in, gram_out, gram_in,
    load_sem, halo_send, halo_recv, mate_send, mate_recv, cross_send, cross_recv, step_send, step_recv, gram_send, gram_recv, const_sem) = refs
    snap, slab = lax.axis_index("snap"), lax.axis_index("slab")
    slabs = lax.axis_size("slab")
    core, chip = snap % 2, snap // 2
    has_lo, has_hi = slab > 0, slab < slabs - 1
    lo_peer = (snap, jnp.maximum(slab - 1, 0))
    hi_peer = (snap, jnp.minimum(slab + 1, slabs - 1))
    mate_peer = (chip * 2 + 1 - core, slab)
    cross_peer = ((1 - chip) * 2 + core, slab)
    snap_peers = [((snap + d) % 4, slab) for d in (1, 2, 3)]

    def zone(i):
        side = (chip + 1 - i // 2) % 2
        return pl.ds(pl.multiple_of((side * 2 + (core + 1 + i) % 2) * LANES, LANES), LANES)

    load = pltpu.make_async_copy(vel_hbm, vel, load_sem)
    load.start()
    bins_load = pltpu.make_async_copy(bins_hbm, bins, const_sem)
    bins_load.start()

    barrier = pltpu.get_barrier_semaphore()
    for peer in snap_peers:
        pl.semaphore_signal(barrier, inc=1, device_id=peer, device_id_type=MESH)
    for cond, peer in ((has_lo, lo_peer), (has_hi, hi_peer)):
        @pl.when(cond)
        def _(peer=peer):
            pl.semaphore_signal(barrier, inc=1, device_id=peer, device_id_type=MESH)
    pl.semaphore_wait(barrier, 3 + has_lo.astype(jnp.int32) + has_hi.astype(jnp.int32))

    def halo_copy(i, side):
        planes = pl.ds(NP - 2, 2) if side == 0 else pl.ds(0, 2)
        return pltpu.make_async_remote_copy(
            src_ref=vel_hbm.at[:, pl.ds(1, 2), planes, :, zone(i)],
            dst_ref=halo.at[i, :, :, side],
            send_sem=halo_send.at[i, side],
            recv_sem=halo_recv.at[i, side],
            device_id=hi_peer if side == 0 else lo_peer,
            device_id_type=MESH,
        )

    for i in range(4):
        for side, cond in ((0, has_hi), (1, has_lo)):
            @pl.when(cond)
            def _(i=i, side=side):
                halo_copy(i, side).start()

    for side, cond in ((0, has_lo), (1, has_hi)):
        @pl.when(jnp.logical_not(cond))
        def _(side=side):
            for i in range(4):
                halo[i, :, :, side] = jnp.zeros((NS, 2, 2, NY, LANES), jnp.bfloat16)

    fill_stencils(*consts)
    bins_load.wait()
    zero = jnp.zeros((8, LANES), jnp.float32)

    def weigh(s, g):
        angle = (jnp.full((8, LANES), bins[s], jnp.int32).astype(jnp.float32) + 0.5) * (
            2.0 * np.pi / BINS
        )
        c, n = jnp.cos(angle), jnp.sin(angle)
        weights[0, s] = c
        weights[1, s] = n
        return (g[0] + c, g[1] + n, g[2] + c * c, g[3] + c * n, g[4] + n * n)

    steps[...] = jnp.zeros((3, 16, LANES), jnp.float32)
    for n, value in enumerate(lax.fori_loop(0, NS, weigh, (zero,) * 5)):
        gram_out[n] = value

    def gram_copy(d):
        return pltpu.make_async_remote_copy(
            src_ref=gram_out, dst_ref=gram_in.at[d],
            send_sem=gram_send.at[d], recv_sem=gram_recv.at[d],
            device_id=snap_peers[d], device_id_type=MESH,
        )

    load.wait()

    def derive(i, p):
        z = zone(i)
        planes = PLANES[p]

        def own(s, comp):
            if p == 0:
                return vel[s, comp, 2:6].reshape(64, NZ)
            return jnp.concatenate([vel[s, comp, 0:2], vel[s, comp, 6:8]], axis=0).reshape(64, NZ)

        def body(s, carry):
            uv = jnp.concatenate([own(s, 0), own(s, 1)], axis=0)
            dz = dot(uv, right_z[:, z])
            v_u = jnp.concatenate(
                [vel[s, 1, :, :, z].reshape(NP * NY, LANES), vel[s, 0, :, :, z].reshape(NP * NY, LANES)],
                axis=0,
            )
            w = vel[s, 2, :, :, z].reshape(NP * NY, LANES)
            from_w = dot(left_w[p], w)
            om_z = dot(left_vu[p], v_u)
            om_x = from_w[:64] - dz[64:]
            om_y = from_w[64:] + dz[:64]
            if p == 1:
                v_halo = halo[i, s, 0].reshape(64, LANES)
                w_halo = halo[i, s, 1].reshape(64, LANES)
                om_z = om_z + dot(left_halo[...], v_halo)
                om_y = om_y - dot(left_halo[...], w_halo)
            omega[s, 0] = om_x.reshape(8, 8, LANES)
            omega[s, 1] = om_y.reshape(8, 8, LANES)
            omega[s, 2] = om_z.reshape(8, 8, LANES)
            return carry

        lax.fori_loop(0, NS, body, 0)

    def accumulate(i, p):
        def body(t, carry):
            c, r = t // 4, t % 4
            rows = pl.ds(2 * r, 2)
            acc = [[None] * 4 for _ in range(3)]
            for s in range(NS):
                om = omega[s, c, rows]
                sq = om * om
                powers = (om, sq, sq * om, sq * sq)
                for k in range(4):
                    for j in range(3):
                        term = powers[k] if j == 0 else weights[j - 1, s][None] * powers[k]
                        acc[j][k] = term if s == 0 else acc[j][k] + term
            for j in range(3):
                for k in range(4):
                    sums[i, p, j, c * 4 + k, rows] = acc[j][k]
            return carry

        lax.fori_loop(0, 12, body, 0)

    def mate_copy(half, p):
        return pltpu.make_async_remote_copy(
            src_ref=sums.at[2 * half, p], dst_ref=mate.at[half, p],
            send_sem=mate_send.at[half, p], recv_sem=mate_recv.at[half, p],
            device_id=mate_peer, device_id_type=MESH,
        )

    def cross_copy(p):
        return pltpu.make_async_remote_copy(
            src_ref=cross_out.at[p], dst_ref=cross_in.at[p],
            send_sem=cross_send.at[p], recv_sem=cross_recv.at[p],
            device_id=cross_peer, device_id_type=MESH,
        )

    def step_copy(p):
        return pltpu.make_async_remote_copy(
            src_ref=step_out.at[p], dst_ref=step_in.at[p],
            send_sem=step_send.at[p], recv_sem=step_recv.at[p],
            device_id=cross_peer, device_id_type=MESH,
        )

    for p in range(2):
        for i in range(4):
            if p == 1:
                for side, cond, gone in ((0, has_lo, has_hi), (1, has_hi, has_lo)):
                    @pl.when(cond)
                    def _(i=i, side=side):
                        halo_copy(i, side).wait_recv()
            derive(i, p)
            accumulate(i, p)
            if p == 0 and i == 0:
                for d in range(3):
                    gram_copy(d).start()
            if i % 2 == 0:
                mate_copy(i // 2, p).start()
            if i == 1:
                mate_copy(0, p).wait_recv()

                def add(t, carry, p=p):
                    for j in range(3):
                        total = sums[1, p, j, t] + mate[0, p, j, t]
                        top = jnp.maximum(jnp.max(jnp.abs(total), axis=(0, 1))[None], 1e-32)
                        step = (top * ((1.0 + 2.0**-7) / TOP)).astype(jnp.bfloat16).astype(jnp.float32)
                        code = jnp.round(total * (1.0 / step)[None]).astype(jnp.int32)
                        cross_out[p, j, t] = code.astype(jnp.int16).reshape(4, NY, LANES)
                        steps[j, pl.ds(t, 1)] = step
                    return carry

                lax.fori_loop(0, 12, add, 0)
                step_out[p] = steps[...].astype(jnp.bfloat16)
                step_copy(p).start()
                cross_copy(p).start()

    for d in range(3):
        gram_copy(d).wait()
    g = [gram_out[n] + gram_in[0, n] + gram_in[1, n] + gram_in[2, n] for n in range(5)]
    g00 = jnp.full((8, LANES), 4.0 * NS, jnp.float32)
    g01, g02, g11, g12, g22 = g
    c00 = g11 * g22 - g12 * g12
    c01 = g02 * g12 - g01 * g22
    c02 = g01 * g12 - g02 * g11
    c11 = g00 * g22 - g02 * g02
    c12 = g02 * g01 - g00 * g12
    c22 = g00 * g11 - g01 * g01
    det = g00 * c00 + g01 * c01 + g02 * c02
    inverse = [[x / det for x in row] for row in ((c00, c01, c02), (c01, c11, c12), (c02, c12, c22))]

    for p in range(2):
        mate_copy(1, p).wait_recv()
        step_copy(p).wait_recv()
        steps[...] = step_in[p].astype(jnp.float32)
        cross_copy(p).wait_recv()

        def solve(t, carry, p=p):
            total = [
                sums[3, p, j, t]
                + mate[1, p, j, t]
                + cross_in[p, j, t].astype(jnp.int32).astype(jnp.float32).reshape(8, 8, LANES)
                * steps[j, pl.ds(t, 1)][None]
                for j in range(3)
            ]
            for n in range(3):
                fit = sum(inverse[n][j][None] * total[j] for j in range(3)).reshape(4, NY, LANES)
                if p == 0:
                    out[n, t // 4, t % 4, 2:6] = fit
                else:
                    out[n, t // 4, t % 4, 0:2] = fit[:2]
                    out[n, t // 4, t % 4, 6:8] = fit[2:]
            return carry

        lax.fori_loop(0, 12, solve, 0)

    for i in range(4):
        for side, cond in ((0, has_hi), (1, has_lo)):
            @pl.when(cond)
            def _(i=i, side=side):
                halo_copy(i, side).wait_send()
    for p in range(2):
        cross_copy(p).wait_send()
        step_copy(p).wait_send()
        for half in range(2):
            mate_copy(half, p).wait_send()


def local(velocity, phase_bins):
    hbm = pl.BlockSpec(memory_space=pltpu.HBM)
    f32, bf16, dma = jnp.float32, jnp.bfloat16, pltpu.SemaphoreType.DMA
    block = (3, 12, 8, 8, LANES)
    return pl.pallas_call(
        kernel,
        out_shape=pltpu.VMEM((3, 3, 4, NP, NY, LANES), f32),
        in_specs=[hbm] * 2,
        out_specs=pl.BlockSpec(memory_space=pltpu.VMEM),
        scratch_shapes=[pltpu.VMEM(c, bf16) for c in ((2, 128, 128), (2, 64, 256), (64, 64), (NZ, NZ))]
        + [
            pltpu.SMEM((NS,), jnp.int32),
            pltpu.VMEM((NS, 3, NP, NY, NZ), bf16),
            pltpu.VMEM((4, NS, 2, 2, 2, NY, LANES), bf16),
            pltpu.VMEM((NS, 3, 8, 8, LANES), f32),
            pltpu.VMEM((2, NS, 8, LANES), f32),
            pltpu.VMEM((4, 2) + block, f32),
            pltpu.VMEM((2, 2) + block, f32),
            pltpu.VMEM((2, 3, 12, 4, NY, LANES), jnp.int16),
            pltpu.VMEM((2, 3, 12, 4, NY, LANES), jnp.int16),
            pltpu.VMEM((3, 16, LANES), f32),
            pltpu.VMEM((2, 3, 16, LANES), bf16),
            pltpu.VMEM((2, 3, 16, LANES), bf16),
            pltpu.VMEM((5, 8, LANES), f32),
            pltpu.VMEM((3, 5, 8, LANES), f32),
            dma, dma((4, 2)), dma((4, 2)), dma((2, 2)), dma((2, 2)), dma((2,)), dma((2,)), dma((2,)), dma((2,)), dma((3,)), dma((3,)), dma,
        ],
        compiler_params=pltpu.CompilerParams(collective_id=0, has_side_effects=True),
    )(velocity, phase_bins)


def solution(mesh):
    in_specs = (P("snap", None, "slab", None, None), P("snap"))
    out_specs = P(None, None, None, "slab", None, "snap")
    return jax.shard_map(local, mesh=mesh, in_specs=in_specs, out_specs=out_specs, check_vma=False)
```

```python
import functools

import jax
import jax.numpy as jnp
import numpy as np
from jax import lax
from jax.experimental import pallas as pl
from jax.experimental.pallas import tpu as pltpu
from jax.sharding import PartitionSpec as P

MESH = pl.DeviceIdType.MESH
BINS = 180
NEAR = 0.75 * 8.0 / 12.0
WIDE = 0.75 / 12.0
PLANES = ((2, 3, 4, 5), (0, 1, 6, 7))
NS, NP, NY, NZ = 16, 8, 16, 512
LANES = 128
TOP = 32766.0


def band(d):
    near = jnp.where(d == 1, NEAR, jnp.where(d == -1, -NEAR, 0.0))
    return near + jnp.where(d == 2, -WIDE, jnp.where(d == -2, WIDE, 0.0))


def grid(rows, cols):
    return [lax.broadcasted_iota(jnp.int32, (rows, cols), n) for n in (0, 1)]


def fill_stencils(left_w, left_vu, left_halo, right_z):
    bf16 = jnp.bfloat16
    for p in range(2):
        r, c = grid(64, NP * NY)
        plane = (r >> 4) + (2 if p == 0 else (r >> 5) * 4)
        same_y, same_x = (r & 15) == (c & 15), plane == (c >> 4)
        dx = jnp.where(same_y, band((c >> 4) - plane), 0.0)
        dy = jnp.where(same_x, band((c & 15) - (r & 15)), 0.0)
        left_w[p, 0:64] = dy.astype(bf16)
        left_w[p, 64:128] = (-dx).astype(bf16)
        left_vu[p, :, 0:128] = dx.astype(bf16)
        left_vu[p, :, 128:256] = (-dy).astype(bf16)
    r, c = grid(64, 64)
    plane = (r >> 4) + (r >> 5) * 4
    beyond = (c >> 4) - 2 + (c >> 5) * 8
    left_halo[...] = jnp.where((r & 15) == (c & 15), band(beyond - plane), 0.0).astype(bf16)
    r, c = grid(NZ, NZ)
    right_z[...] = band(r - c).astype(bf16)


def dot(a, b):
    return jnp.dot(a, b, preferred_element_type=jnp.float32)


def kernel(
    vel_hbm, bins_hbm, out, *refs):
    consts, refs = refs[:4], refs[4:]
    left_w, left_vu, left_halo, right_z = consts
    (bins, vel, halo, omega, weights, sums, mate, cross_out, cross_in, steps, step_out, step_in, gram_out, gram_in,
    load_sem, halo_send, halo_recv, mate_send, mate_recv, cross_send, cross_recv, step_send, step_recv, gram_send, gram_recv, const_sem) = refs
    snap, slab = lax.axis_index("snap"), lax.axis_index("slab")
    slabs = lax.axis_size("slab")
    core, chip = snap % 2, snap // 2
    has_lo, has_hi = slab > 0, slab < slabs - 1
    lo_peer = (snap, jnp.maximum(slab - 1, 0))
    hi_peer = (snap, jnp.minimum(slab + 1, slabs - 1))
    mate_peer = (chip * 2 + 1 - core, slab)
    cross_peer = ((1 - chip) * 2 + core, slab)
    snap_peers = [((snap + d) % 4, slab) for d in (1, 2, 3)]

    def zone(i):
        side = (chip + 1 - i // 2) % 2
        return pl.ds(pl.multiple_of((side * 2 + (core + 1 + i) % 2) * LANES, LANES), LANES)

    load = pltpu.make_async_copy(vel_hbm, vel, load_sem)
    load.start()
    bins_load = pltpu.make_async_copy(bins_hbm, bins, const_sem)
    bins_load.start()

    barrier = pltpu.get_barrier_semaphore()
    for peer in snap_peers:
        pl.semaphore_signal(barrier, inc=1, device_id=peer, device_id_type=MESH)
    for cond, peer in ((has_lo, lo_peer), (has_hi, hi_peer)):
        @pl.when(cond)
        def _(peer=peer):
            pl.semaphore_signal(barrier, inc=1, device_id=peer, device_id_type=MESH)
    pl.semaphore_wait(barrier, 3 + has_lo.astype(jnp.int32) + has_hi.astype(jnp.int32))

    def halo_copy(i, side):
        planes = pl.ds(NP - 2, 2) if side == 0 else pl.ds(0, 2)
        return pltpu.make_async_remote_copy(
            src_ref=vel_hbm.at[:, pl.ds(1, 2), planes, :, zone(i)],
            dst_ref=halo.at[i, :, :, side],
            send_sem=halo_send.at[i, side],
            recv_sem=halo_recv.at[i, side],
            device_id=hi_peer if side == 0 else lo_peer,
            device_id_type=MESH,
        )

    for i in range(4):
        for side, cond in ((0, has_hi), (1, has_lo)):
            @pl.when(cond)
            def _(i=i, side=side):
                halo_copy(i, side).start()

    for side, cond in ((0, has_lo), (1, has_hi)):
        @pl.when(jnp.logical_not(cond))
        def _(side=side):
            for i in range(4):
                halo[i, :, :, side] = jnp.zeros((NS, 2, 2, NY, LANES), jnp.bfloat16)

    fill_stencils(*consts)
    bins_load.wait()
    zero = jnp.zeros((8, LANES), jnp.float32)

    def weigh(s, g):
        angle = (jnp.full((8, LANES), bins[s], jnp.int32).astype(jnp.float32) + 0.5) * (
            2.0 * np.pi / BINS
        )
        c, n = jnp.cos(angle), jnp.sin(angle)
        weights[0, s] = c
        weights[1, s] = n
        return (g[0] + c, g[1] + n, g[2] + c * c, g[3] + c * n, g[4] + n * n)

    steps[...] = jnp.zeros((3, 16, LANES), jnp.float32)
    for n, value in enumerate(lax.fori_loop(0, NS, weigh, (zero,) * 5)):
        gram_out[n] = value

    def gram_copy(d):
        return pltpu.make_async_remote_copy(
            src_ref=gram_out, dst_ref=gram_in.at[d],
            send_sem=gram_send.at[d], recv_sem=gram_recv.at[d],
            device_id=snap_peers[d], device_id_type=MESH,
        )

    load.wait()

    def derive(i, p):
        z = zone(i)
        planes = PLANES[p]

        def own(s, comp):
            if p == 0:
                return vel[s, comp, 2:6].reshape(64, NZ)
            return jnp.concatenate([vel[s, comp, 0:2], vel[s, comp, 6:8]], axis=0).reshape(64, NZ)

        def body(s, carry):
            uv = jnp.concatenate([own(s, 0), own(s, 1)], axis=0)
            dz = dot(uv, right_z[:, z])
            v_u = jnp.concatenate(
                [vel[s, 1, :, :, z].reshape(NP * NY, LANES), vel[s, 0, :, :, z].reshape(NP * NY, LANES)],
                axis=0,
            )
            w = vel[s, 2, :, :, z].reshape(NP * NY, LANES)
            from_w = dot(left_w[p], w)
            om_z = dot(left_vu[p], v_u)
            om_x = from_w[:64] - dz[64:]
            om_y = from_w[64:] + dz[:64]
            if p == 1:
                v_halo = halo[i, s, 0].reshape(64, LANES)
                w_halo = halo[i, s, 1].reshape(64, LANES)
                om_z = om_z + dot(left_halo[...], v_halo)
                om_y = om_y - dot(left_halo[...], w_halo)
            omega[s, 0] = om_x.reshape(8, 8, LANES)
            omega[s, 1] = om_y.reshape(8, 8, LANES)
            omega[s, 2] = om_z.reshape(8, 8, LANES)
            return carry

        lax.fori_loop(0, NS, body, 0)

    def accumulate(i, p):
        def body(t, carry):
            c, r = t // 4, t % 4
            rows = pl.ds(2 * r, 2)
            acc = [[None] * 4 for _ in range(3)]
            for s in range(NS):
                om = omega[s, c, rows]
                sq = om * om
                powers = (om, sq, sq * om, sq * sq)
                for k in range(4):
                    for j in range(3):
                        term = powers[k] if j == 0 else weights[j - 1, s][None] * powers[k]
                        acc[j][k] = term if s == 0 else acc[j][k] + term
            for j in range(3):
                for k in range(4):
                    sums[i, p, j, c * 4 + k, rows] = acc[j][k]
            return carry

        lax.fori_loop(0, 12, body, 0)

    def mate_copy(half, p):
        return pltpu.make_async_remote_copy(
            src_ref=sums.at[2 * half, p], dst_ref=mate.at[half, p],
            send_sem=mate_send.at[half, p], recv_sem=mate_recv.at[half, p],
            device_id=mate_peer, device_id_type=MESH,
        )

    def cross_copy(p, c):
        part = pl.ds(4 * c, 4)
        return pltpu.make_async_remote_copy(
            src_ref=cross_out.at[p, :, part], dst_ref=cross_in.at[p, :, part],
            send_sem=cross_send.at[p, c], recv_sem=cross_recv.at[p, c],
            device_id=cross_peer, device_id_type=MESH,
        )

    def step_copy(p):
        return pltpu.make_async_remote_copy(
            src_ref=step_out.at[p], dst_ref=step_in.at[p],
            send_sem=step_send.at[p], recv_sem=step_recv.at[p],
            device_id=cross_peer, device_id_type=MESH,
        )

    for p in range(2):
        for i in range(4):
            if p == 1:
                for side, cond, gone in ((0, has_lo, has_hi), (1, has_hi, has_lo)):
                    @pl.when(cond)
                    def _(i=i, side=side):
                        halo_copy(i, side).wait_recv()
            derive(i, p)
            accumulate(i, p)
            if p == 0 and i == 0:
                for d in range(3):
                    gram_copy(d).start()
            if i % 2 == 0:
                mate_copy(i // 2, p).start()
            if i == 1:
                mate_copy(0, p).wait_recv()

                def add(t, carry, p=p):
                    for j in range(3):
                        total = sums[1, p, j, t] + mate[0, p, j, t]
                        top = jnp.maximum(jnp.max(jnp.abs(total), axis=(0, 1))[None], 1e-32)
                        step = (top * ((1.0 + 2.0**-7) / TOP)).astype(jnp.bfloat16).astype(jnp.float32)
                        code = jnp.round(total * (1.0 / step)[None]).astype(jnp.int32)
                        cross_out[p, j, t] = code.astype(jnp.int16).reshape(4, NY, LANES)
                        steps[j, pl.ds(t, 1)] = step
                    return carry

                lax.fori_loop(0, 12, add, 0)
                step_out[p] = steps[...].astype(jnp.bfloat16)
                step_copy(p).start()
                for c in range(3):
                    cross_copy(p, c).start()

    for d in range(3):
        gram_copy(d).wait()
    g = [gram_out[n] + gram_in[0, n] + gram_in[1, n] + gram_in[2, n] for n in range(5)]
    g00 = jnp.full((8, LANES), 4.0 * NS, jnp.float32)
    g01, g02, g11, g12, g22 = g
    c00 = g11 * g22 - g12 * g12
    c01 = g02 * g12 - g01 * g22
    c02 = g01 * g12 - g02 * g11
    c11 = g00 * g22 - g02 * g02
    c12 = g02 * g01 - g00 * g12
    c22 = g00 * g11 - g01 * g01
    det = g00 * c00 + g01 * c01 + g02 * c02
    inverse = [[x / det for x in row] for row in ((c00, c01, c02), (c01, c11, c12), (c02, c12, c22))]

    for p in range(2):
        mate_copy(1, p).wait_recv()

        def fold(t, carry, p=p):
            for j in range(3):
                sums[3, p, j, t] = sums[3, p, j, t] + mate[1, p, j, t]
            return carry

        lax.fori_loop(0, 12, fold, 0)
    for p in range(2):
        step_copy(p).wait_recv()
        steps[...] = step_in[p].astype(jnp.float32)

        def solve(t, carry, p=p):
            total = [
                sums[3, p, j, t]
                + cross_in[p, j, t].astype(jnp.int32).astype(jnp.float32).reshape(8, 8, LANES)
                * steps[j, pl.ds(t, 1)][None]
                for j in range(3)
            ]
            for n in range(3):
                fit = sum(inverse[n][j][None] * total[j] for j in range(3)).reshape(4, NY, LANES)
                if p == 0:
                    out[n, t // 4, t % 4, 2:6] = fit
                else:
                    out[n, t // 4, t % 4, 0:2] = fit[:2]
                    out[n, t // 4, t % 4, 6:8] = fit[2:]
            return carry

        for c in range(3):
            cross_copy(p, c).wait_recv()
            lax.fori_loop(4 * c, 4 * c + 4, solve, 0)

    for i in range(4):
        for side, cond in ((0, has_hi), (1, has_lo)):
            @pl.when(cond)
            def _(i=i, side=side):
                halo_copy(i, side).wait_send()
    for p in range(2):
        for c in range(3):
            cross_copy(p, c).wait_send()
        step_copy(p).wait_send()
        for half in range(2):
            mate_copy(half, p).wait_send()


def local(velocity, phase_bins):
    hbm = pl.BlockSpec(memory_space=pltpu.HBM)
    f32, bf16, dma = jnp.float32, jnp.bfloat16, pltpu.SemaphoreType.DMA
    block = (3, 12, 8, 8, LANES)
    return pl.pallas_call(
        kernel,
        out_shape=pltpu.VMEM((3, 3, 4, NP, NY, LANES), f32),
        in_specs=[hbm] * 2,
        out_specs=pl.BlockSpec(memory_space=pltpu.VMEM),
        scratch_shapes=[pltpu.VMEM(c, bf16) for c in ((2, 128, 128), (2, 64, 256), (64, 64), (NZ, NZ))]
        + [
            pltpu.SMEM((NS,), jnp.int32),
            pltpu.VMEM((NS, 3, NP, NY, NZ), bf16),
            pltpu.VMEM((4, NS, 2, 2, 2, NY, LANES), bf16),
            pltpu.VMEM((NS, 3, 8, 8, LANES), f32),
            pltpu.VMEM((2, NS, 8, LANES), f32),
            pltpu.VMEM((4, 2) + block, f32),
            pltpu.VMEM((2, 2) + block, f32),
            pltpu.VMEM((2, 3, 12, 4, NY, LANES), jnp.int16),
            pltpu.VMEM((2, 3, 12, 4, NY, LANES), jnp.int16),
            pltpu.VMEM((3, 16, LANES), f32),
            pltpu.VMEM((2, 3, 16, LANES), bf16),
            pltpu.VMEM((2, 3, 16, LANES), bf16),
            pltpu.VMEM((5, 8, LANES), f32),
            pltpu.VMEM((3, 5, 8, LANES), f32),
            dma, dma((4, 2)), dma((4, 2)), dma((2, 2)), dma((2, 2)), dma((2, 3)), dma((2, 3)), dma((2,)), dma((2,)), dma((3,)), dma((3,)), dma,
        ],
        compiler_params=pltpu.CompilerParams(collective_id=0, has_side_effects=True),
    )(velocity, phase_bins)


def solution(mesh):
    in_specs = (P("snap", None, "slab", None, None), P("snap"))
    out_specs = P(None, None, None, "slab", None, "snap")
    return jax.shard_map(local, mesh=mesh, in_specs=in_specs, out_specs=out_specs, check_vma=False)
```

```python
import functools

import jax
import jax.numpy as jnp
import numpy as np
from jax import lax
from jax.experimental import pallas as pl
from jax.experimental.pallas import tpu as pltpu
from jax.sharding import PartitionSpec as P

MESH = pl.DeviceIdType.MESH
BINS = 180
NEAR = 0.75 * 8.0 / 12.0
WIDE = 0.75 / 12.0
PLANES = ((2, 3, 4, 5), (0, 1, 6, 7))
NS, NP, NY, NZ = 16, 8, 16, 512
LANES = 128
TOP = 32766.0


def band(d):
    near = jnp.where(d == 1, NEAR, jnp.where(d == -1, -NEAR, 0.0))
    return near + jnp.where(d == 2, -WIDE, jnp.where(d == -2, WIDE, 0.0))


def grid(rows, cols):
    return [lax.broadcasted_iota(jnp.int32, (rows, cols), n) for n in (0, 1)]


def fill_stencils(left_w, left_vu, left_halo, right_z):
    bf16 = jnp.bfloat16
    for p in range(2):
        r, c = grid(64, NP * NY)
        plane = (r >> 4) + (2 if p == 0 else (r >> 5) * 4)
        same_y, same_x = (r & 15) == (c & 15), plane == (c >> 4)
        dx = jnp.where(same_y, band((c >> 4) - plane), 0.0)
        dy = jnp.where(same_x, band((c & 15) - (r & 15)), 0.0)
        left_w[p, 0:64] = dy.astype(bf16)
        left_w[p, 64:128] = (-dx).astype(bf16)
        left_vu[p, :, 0:128] = dx.astype(bf16)
        left_vu[p, :, 128:256] = (-dy).astype(bf16)
    r, c = grid(64, 64)
    plane = (r >> 4) + (r >> 5) * 4
    beyond = (c >> 4) - 2 + (c >> 5) * 8
    left_halo[...] = jnp.where((r & 15) == (c & 15), band(beyond - plane), 0.0).astype(bf16)
    r, c = grid(NZ, NZ)
    right_z[...] = band(r - c).astype(bf16)


def dot(a, b):
    return jnp.dot(a, b, preferred_element_type=jnp.float32)


def kernel(
    vel_hbm, bins_hbm, out, *refs):
    consts, refs = refs[:4], refs[4:]
    left_w, left_vu, left_halo, right_z = consts
    (bins, vel, halo, omega, weights, sums, mate, cross_out, cross_in, steps, step_out, step_in, gram_out, gram_in,
    load_sem, halo_send, halo_recv, mate_send, mate_recv, cross_send, cross_recv, step_send, step_recv, gram_send, gram_recv, const_sem) = refs
    snap, slab = lax.axis_index("snap"), lax.axis_index("slab")
    slabs = lax.axis_size("slab")
    core, chip = snap % 2, snap // 2
    has_lo, has_hi = slab > 0, slab < slabs - 1
    lo_peer = (snap, jnp.maximum(slab - 1, 0))
    hi_peer = (snap, jnp.minimum(slab + 1, slabs - 1))
    mate_peer = (chip * 2 + 1 - core, slab)
    cross_peer = ((1 - chip) * 2 + core, slab)
    snap_peers = [((snap + d) % 4, slab) for d in (1, 2, 3)]

    def zone(i):
        side = (chip + 1 - i // 2) % 2
        return pl.ds(pl.multiple_of((side * 2 + (core + 1 + i) % 2) * LANES, LANES), LANES)

    load = pltpu.make_async_copy(vel_hbm, vel, load_sem)
    load.start()
    bins_load = pltpu.make_async_copy(bins_hbm, bins, const_sem)
    bins_load.start()

    barrier = pltpu.get_barrier_semaphore()
    for peer in snap_peers:
        pl.semaphore_signal(barrier, inc=1, device_id=peer, device_id_type=MESH)
    for cond, peer in ((has_lo, lo_peer), (has_hi, hi_peer)):
        @pl.when(cond)
        def _(peer=peer):
            pl.semaphore_signal(barrier, inc=1, device_id=peer, device_id_type=MESH)
    pl.semaphore_wait(barrier, 3 + has_lo.astype(jnp.int32) + has_hi.astype(jnp.int32))

    def halo_copy(i, side):
        planes = pl.ds(NP - 2, 2) if side == 0 else pl.ds(0, 2)
        return pltpu.make_async_remote_copy(
            src_ref=vel_hbm.at[:, pl.ds(1, 2), planes, :, zone(i)],
            dst_ref=halo.at[i, :, :, side],
            send_sem=halo_send.at[i, side],
            recv_sem=halo_recv.at[i, side],
            device_id=hi_peer if side == 0 else lo_peer,
            device_id_type=MESH,
        )

    for i in range(4):
        for side, cond in ((0, has_hi), (1, has_lo)):
            @pl.when(cond)
            def _(i=i, side=side):
                halo_copy(i, side).start()

    for side, cond in ((0, has_lo), (1, has_hi)):
        @pl.when(jnp.logical_not(cond))
        def _(side=side):
            for i in range(4):
                halo[i, :, :, side] = jnp.zeros((NS, 2, 2, NY, LANES), jnp.bfloat16)

    fill_stencils(*consts)
    bins_load.wait()
    zero = jnp.zeros((8, LANES), jnp.float32)

    def weigh(s, g):
        angle = (jnp.full((8, LANES), bins[s], jnp.int32).astype(jnp.float32) + 0.5) * (
            2.0 * np.pi / BINS
        )
        c, n = jnp.cos(angle), jnp.sin(angle)
        weights[0, s] = c
        weights[1, s] = n
        return (g[0] + c, g[1] + n, g[2] + c * c, g[3] + c * n, g[4] + n * n)

    steps[...] = jnp.zeros((3, 16, LANES), jnp.float32)
    for n, value in enumerate(lax.fori_loop(0, NS, weigh, (zero,) * 5)):
        gram_out[n] = value

    def gram_copy(d):
        return pltpu.make_async_remote_copy(
            src_ref=gram_out, dst_ref=gram_in.at[d],
            send_sem=gram_send.at[d], recv_sem=gram_recv.at[d],
            device_id=snap_peers[d], device_id_type=MESH,
        )

    load.wait()

    def derive(i, p):
        z = zone(i)
        planes = PLANES[p]

        def own(s, comp):
            if p == 0:
                return vel[s, comp, 2:6].reshape(64, NZ)
            return jnp.concatenate([vel[s, comp, 0:2], vel[s, comp, 6:8]], axis=0).reshape(64, NZ)

        def body(s, carry):
            uv = jnp.concatenate([own(s, 0), own(s, 1)], axis=0)
            dz = dot(uv, right_z[:, z])
            v_u = jnp.concatenate(
                [vel[s, 1, :, :, z].reshape(NP * NY, LANES), vel[s, 0, :, :, z].reshape(NP * NY, LANES)],
                axis=0,
            )
            w = vel[s, 2, :, :, z].reshape(NP * NY, LANES)
            from_w = dot(left_w[p], w)
            om_z = dot(left_vu[p], v_u)
            om_x = from_w[:64] - dz[64:]
            om_y = from_w[64:] + dz[:64]
            if p == 1:
                v_halo = halo[i, s, 0].reshape(64, LANES)
                w_halo = halo[i, s, 1].reshape(64, LANES)
                om_z = om_z + dot(left_halo[...], v_halo)
                om_y = om_y - dot(left_halo[...], w_halo)
            omega[s, 0] = om_x.reshape(8, 8, LANES)
            omega[s, 1] = om_y.reshape(8, 8, LANES)
            omega[s, 2] = om_z.reshape(8, 8, LANES)
            return carry

        lax.fori_loop(0, NS, body, 0)

    def accumulate(i, p):
        def body(t, carry):
            c, r = t // 4, t % 4
            rows = pl.ds(2 * r, 2)
            acc = [[None] * 4 for _ in range(3)]
            for s in range(NS):
                om = omega[s, c, rows]
                sq = om * om
                powers = (om, sq, sq * om, sq * sq)
                for k in range(4):
                    for j in range(3):
                        term = powers[k] if j == 0 else weights[j - 1, s][None] * powers[k]
                        acc[j][k] = term if s == 0 else acc[j][k] + term
            for j in range(3):
                for k in range(4):
                    sums[i, p, j, c * 4 + k, rows] = acc[j][k]
            return carry

        lax.fori_loop(0, 12, body, 0)

    def mate_copy(half, p):
        return pltpu.make_async_remote_copy(
            src_ref=sums.at[2 * half, p], dst_ref=mate.at[half, p],
            send_sem=mate_send.at[half, p], recv_sem=mate_recv.at[half, p],
            device_id=mate_peer, device_id_type=MESH,
        )

    def cross_copy(p):
        return pltpu.make_async_remote_copy(
            src_ref=cross_out.at[p], dst_ref=cross_in.at[p],
            send_sem=cross_send.at[p], recv_sem=cross_recv.at[p],
            device_id=cross_peer, device_id_type=MESH,
        )

    def step_copy(p):
        return pltpu.make_async_remote_copy(
            src_ref=step_out.at[p], dst_ref=step_in.at[p],
            send_sem=step_send.at[p], recv_sem=step_recv.at[p],
            device_id=cross_peer, device_id_type=MESH,
        )

    for p in range(2):
        for i in range(4):
            if p == 1:
                for side, cond, gone in ((0, has_lo, has_hi), (1, has_hi, has_lo)):
                    @pl.when(cond)
                    def _(i=i, side=side):
                        halo_copy(i, side).wait_recv()
            derive(i, p)
            accumulate(i, p)
            if p == 0 and i == 0:
                for d in range(3):
                    gram_copy(d).start()
            if i % 2 == 0:
                mate_copy(i // 2, p).start()
            if i == 1:
                mate_copy(0, p).wait_recv()

                def add(t, carry, p=p):
                    for j in range(3):
                        total = sums[1, p, j, t] + mate[0, p, j, t]
                        top = jnp.maximum(jnp.max(jnp.abs(total), axis=(0, 1))[None], 1e-32)
                        step = (top * ((1.0 + 2.0**-7) / TOP)).astype(jnp.bfloat16).astype(jnp.float32)
                        code = jnp.round(total * (1.0 / step)[None]).astype(jnp.int32)
                        cross_out[p, j, t] = code.astype(jnp.int16).reshape(4, NY, LANES)
                        steps[j, pl.ds(t, 1)] = step
                    return carry

                lax.fori_loop(0, 12, add, 0)
                step_out[p] = steps[...].astype(jnp.bfloat16)
                step_copy(p).start()
                cross_copy(p).start()

    for d in range(3):
        gram_copy(d).wait()
    g = [gram_out[n] + gram_in[0, n] + gram_in[1, n] + gram_in[2, n] for n in range(5)]
    g00 = jnp.full((8, LANES), 4.0 * NS, jnp.float32)
    g01, g02, g11, g12, g22 = g
    c00 = g11 * g22 - g12 * g12
    c01 = g02 * g12 - g01 * g22
    c02 = g01 * g12 - g02 * g11
    c11 = g00 * g22 - g02 * g02
    c12 = g02 * g01 - g00 * g12
    c22 = g00 * g11 - g01 * g01
    det = g00 * c00 + g01 * c01 + g02 * c02
    inverse = [[x / det for x in row] for row in ((c00, c01, c02), (c01, c11, c12), (c02, c12, c22))]

    for p in range(2):
        mate_copy(1, p).wait_recv()
        step_copy(p).wait_recv()
        steps[...] = step_in[p].astype(jnp.float32)
        cross_copy(p).wait_recv()

        def solve(t, carry, p=p):
            total = [
                sums[3, p, j, t]
                + mate[1, p, j, t]
                + cross_in[p, j, t].astype(jnp.int32).astype(jnp.float32).reshape(8, 8, LANES)
                * steps[j, pl.ds(t, 1)][None]
                for j in range(3)
            ]
            for n in range(3):
                fit = sum(inverse[n][j][None] * total[j] for j in range(3)).reshape(4, NY, LANES)
                if p == 0:
                    out[n, t // 4, t % 4, 2:6] = fit
                else:
                    out[n, t // 4, t % 4, 0:2] = fit[:2]
                    out[n, t // 4, t % 4, 6:8] = fit[2:]
            return carry

        lax.fori_loop(0, 12, solve, 0)

    for i in range(4):
        for side, cond in ((0, has_hi), (1, has_lo)):
            @pl.when(cond)
            def _(i=i, side=side):
                halo_copy(i, side).wait_send()
    for p in range(2):
        cross_copy(p).wait_send()
        step_copy(p).wait_send()
        for half in range(2):
            mate_copy(half, p).wait_send()


def put(fit, out, sem):
    copies = [
        pltpu.make_async_copy(fit.at[n, m], out.at[n, m], sem.at[n, m]) for n in range(3) for m in range(3)
    ]
    for copy in copies:
        copy.start()
    for copy in copies:
        copy.wait()


def local(velocity, phase_bins):
    hbm = pl.BlockSpec(memory_space=pltpu.HBM)
    f32, bf16, dma = jnp.float32, jnp.bfloat16, pltpu.SemaphoreType.DMA
    block = (3, 12, 8, 8, LANES)
    fit = pl.pallas_call(
        kernel,
        out_shape=pltpu.VMEM((3, 3, 4, NP, NY, LANES), f32),
        in_specs=[hbm] * 2,
        out_specs=pl.BlockSpec(memory_space=pltpu.VMEM),
        scratch_shapes=[pltpu.VMEM(c, bf16) for c in ((2, 128, 128), (2, 64, 256), (64, 64), (NZ, NZ))]
        + [
            pltpu.SMEM((NS,), jnp.int32),
            pltpu.VMEM((NS, 3, NP, NY, NZ), bf16),
            pltpu.VMEM((4, NS, 2, 2, 2, NY, LANES), bf16),
            pltpu.VMEM((NS, 3, 8, 8, LANES), f32),
            pltpu.VMEM((2, NS, 8, LANES), f32),
            pltpu.VMEM((4, 2) + block, f32),
            pltpu.VMEM((2, 2) + block, f32),
            pltpu.VMEM((2, 3, 12, 4, NY, LANES), jnp.int16),
            pltpu.VMEM((2, 3, 12, 4, NY, LANES), jnp.int16),
            pltpu.VMEM((3, 16, LANES), f32),
            pltpu.VMEM((2, 3, 16, LANES), bf16),
            pltpu.VMEM((2, 3, 16, LANES), bf16),
            pltpu.VMEM((5, 8, LANES), f32),
            pltpu.VMEM((3, 5, 8, LANES), f32),
            dma, dma((4, 2)), dma((4, 2)), dma((2, 2)), dma((2, 2)), dma((2,)), dma((2,)), dma((2,)), dma((2,)), dma((3,)), dma((3,)), dma,
        ],
        compiler_params=pltpu.CompilerParams(collective_id=0, has_side_effects=True),
    )(velocity, phase_bins)
    return pl.pallas_call(
        put,
        out_shape=jax.ShapeDtypeStruct(fit.shape, f32),
        in_specs=[pl.BlockSpec(memory_space=pltpu.VMEM)],
        out_specs=hbm,
        scratch_shapes=[dma((3, 3))],
        compiler_params=pltpu.CompilerParams(vmem_limit_bytes=8 * 1024 * 1024),
    )(fit)


def solution(mesh):
    in_specs = (P("snap", None, "slab", None, None), P("snap"))
    out_specs = P(None, None, None, "slab", None, "snap")
    return jax.shard_map(local, mesh=mesh, in_specs=in_specs, out_specs=out_specs, check_vma=False)
```

```python
import functools

import jax
import jax.numpy as jnp
import numpy as np
from jax import lax
from jax.experimental import pallas as pl
from jax.experimental.pallas import tpu as pltpu
from jax.sharding import PartitionSpec as P

MESH = pl.DeviceIdType.MESH
BINS = 180
NEAR = 0.75 * 8.0 / 12.0
WIDE = 0.75 / 12.0
PLANES = ((2, 3, 4, 5), (0, 1, 6, 7))
NS, NP, NY, NZ = 16, 8, 16, 512
LANES = 128
TOP = 32766.0


def band(d):
    near = jnp.where(d == 1, NEAR, jnp.where(d == -1, -NEAR, 0.0))
    return near + jnp.where(d == 2, -WIDE, jnp.where(d == -2, WIDE, 0.0))


def grid(rows, cols):
    return [lax.broadcasted_iota(jnp.int32, (rows, cols), n) for n in (0, 1)]


def fill_stencils(left_w, left_vu, left_halo, right_z):
    bf16 = jnp.bfloat16
    for p in range(2):
        r, c = grid(64, NP * NY)
        plane = (r >> 4) + (2 if p == 0 else (r >> 5) * 4)
        same_y, same_x = (r & 15) == (c & 15), plane == (c >> 4)
        dx = jnp.where(same_y, band((c >> 4) - plane), 0.0)
        dy = jnp.where(same_x, band((c & 15) - (r & 15)), 0.0)
        left_w[p, 0:64] = dy.astype(bf16)
        left_w[p, 64:128] = (-dx).astype(bf16)
        left_vu[p, :, 0:128] = dx.astype(bf16)
        left_vu[p, :, 128:256] = (-dy).astype(bf16)
    r, c = grid(64, 64)
    plane = (r >> 4) + (r >> 5) * 4
    beyond = (c >> 4) - 2 + (c >> 5) * 8
    left_halo[...] = jnp.where((r & 15) == (c & 15), band(beyond - plane), 0.0).astype(bf16)
    r, c = grid(NZ, NZ)
    right_z[...] = band(r - c).astype(bf16)


def dot(a, b):
    return jnp.dot(a, b, preferred_element_type=jnp.float32)


def kernel(
    vel_hbm, bins_hbm, out, *refs):
    consts, refs = refs[:4], refs[4:]
    left_w, left_vu, left_halo, right_z = consts
    (bins, vel, halo, omega, weights, sums, mate, cross_out, cross_in, steps, step_out, step_in, gram_out, gram_in,
    load_sem, halo_send, halo_recv, mate_send, mate_recv, cross_send, cross_recv, step_send, step_recv, gram_send, gram_recv, const_sem) = refs
    snap, slab = lax.axis_index("snap"), lax.axis_index("slab")
    slabs = lax.axis_size("slab")
    core, chip = snap % 2, snap // 2
    has_lo, has_hi = slab > 0, slab < slabs - 1
    lo_peer = (snap, jnp.maximum(slab - 1, 0))
    hi_peer = (snap, jnp.minimum(slab + 1, slabs - 1))
    mate_peer = (chip * 2 + 1 - core, slab)
    cross_peer = ((1 - chip) * 2 + core, slab)
    snap_peers = [((snap + d) % 4, slab) for d in (1, 2, 3)]

    def zone(i):
        side = (chip + 1 - i // 2) % 2
        return pl.ds(pl.multiple_of((side * 2 + (core + 1 + i) % 2) * LANES, LANES), LANES)

    load = pltpu.make_async_copy(vel_hbm, vel, load_sem)
    bins_load = pltpu.make_async_copy(bins_hbm, bins, const_sem)
    bins_load.start()

    barrier = pltpu.get_barrier_semaphore()
    for peer in snap_peers:
        pl.semaphore_signal(barrier, inc=1, device_id=peer, device_id_type=MESH)
    for cond, peer in ((has_lo, lo_peer), (has_hi, hi_peer)):
        @pl.when(cond)
        def _(peer=peer):
            pl.semaphore_signal(barrier, inc=1, device_id=peer, device_id_type=MESH)
    pl.semaphore_wait(barrier, 3 + has_lo.astype(jnp.int32) + has_hi.astype(jnp.int32))

    def halo_copy(i, side):
        planes = pl.ds(NP - 2, 2) if side == 0 else pl.ds(0, 2)
        return pltpu.make_async_remote_copy(
            src_ref=vel_hbm.at[:, pl.ds(1, 2), planes, :, zone(i)],
            dst_ref=halo.at[i, :, :, side],
            send_sem=halo_send.at[i, side],
            recv_sem=halo_recv.at[i, side],
            device_id=hi_peer if side == 0 else lo_peer,
            device_id_type=MESH,
        )

    for i in range(4):
        for side, cond in ((0, has_hi), (1, has_lo)):
            @pl.when(cond)
            def _(i=i, side=side):
                halo_copy(i, side).start()
    load.start()

    for side, cond in ((0, has_lo), (1, has_hi)):
        @pl.when(jnp.logical_not(cond))
        def _(side=side):
            for i in range(4):
                halo[i, :, :, side] = jnp.zeros((NS, 2, 2, NY, LANES), jnp.bfloat16)

    fill_stencils(*consts)
    bins_load.wait()
    zero = jnp.zeros((8, LANES), jnp.float32)

    def weigh(s, g):
        angle = (jnp.full((8, LANES), bins[s], jnp.int32).astype(jnp.float32) + 0.5) * (
            2.0 * np.pi / BINS
        )
        c, n = jnp.cos(angle), jnp.sin(angle)
        weights[0, s] = c
        weights[1, s] = n
        return (g[0] + c, g[1] + n, g[2] + c * c, g[3] + c * n, g[4] + n * n)

    steps[...] = jnp.zeros((3, 16, LANES), jnp.float32)
    for n, value in enumerate(lax.fori_loop(0, NS, weigh, (zero,) * 5)):
        gram_out[n] = value

    def gram_copy(d):
        return pltpu.make_async_remote_copy(
            src_ref=gram_out, dst_ref=gram_in.at[d],
            send_sem=gram_send.at[d], recv_sem=gram_recv.at[d],
            device_id=snap_peers[d], device_id_type=MESH,
        )

    load.wait()

    def derive(i, p):
        z = zone(i)
        planes = PLANES[p]

        def own(s, comp):
            if p == 0:
                return vel[s, comp, 2:6].reshape(64, NZ)
            return jnp.concatenate([vel[s, comp, 0:2], vel[s, comp, 6:8]], axis=0).reshape(64, NZ)

        def body(s, carry):
            uv = jnp.concatenate([own(s, 0), own(s, 1)], axis=0)
            dz = dot(uv, right_z[:, z])
            v_u = jnp.concatenate(
                [vel[s, 1, :, :, z].reshape(NP * NY, LANES), vel[s, 0, :, :, z].reshape(NP * NY, LANES)],
                axis=0,
            )
            w = vel[s, 2, :, :, z].reshape(NP * NY, LANES)
            from_w = dot(left_w[p], w)
            om_z = dot(left_vu[p], v_u)
            om_x = from_w[:64] - dz[64:]
            om_y = from_w[64:] + dz[:64]
            if p == 1:
                v_halo = halo[i, s, 0].reshape(64, LANES)
                w_halo = halo[i, s, 1].reshape(64, LANES)
                om_z = om_z + dot(left_halo[...], v_halo)
                om_y = om_y - dot(left_halo[...], w_halo)
            omega[s, 0] = om_x.reshape(8, 8, LANES)
            omega[s, 1] = om_y.reshape(8, 8, LANES)
            omega[s, 2] = om_z.reshape(8, 8, LANES)
            return carry

        lax.fori_loop(0, NS, body, 0)

    def accumulate(i, p):
        def body(t, carry):
            c, r = t // 4, t % 4
            rows = pl.ds(2 * r, 2)
            acc = [[None] * 4 for _ in range(3)]
            for s in range(NS):
                om = omega[s, c, rows]
                sq = om * om
                powers = (om, sq, sq * om, sq * sq)
                for k in range(4):
                    for j in range(3):
                        term = powers[k] if j == 0 else weights[j - 1, s][None] * powers[k]
                        acc[j][k] = term if s == 0 else acc[j][k] + term
            for j in range(3):
                for k in range(4):
                    sums[i, p, j, c * 4 + k, rows] = acc[j][k]
            return carry

        lax.fori_loop(0, 12, body, 0)

    def mate_copy(half, p):
        return pltpu.make_async_remote_copy(
            src_ref=sums.at[2 * half, p], dst_ref=mate.at[half, p],
            send_sem=mate_send.at[half, p], recv_sem=mate_recv.at[half, p],
            device_id=mate_peer, device_id_type=MESH,
        )

    def cross_copy(p):
        return pltpu.make_async_remote_copy(
            src_ref=cross_out.at[p], dst_ref=cross_in.at[p],
            send_sem=cross_send.at[p], recv_sem=cross_recv.at[p],
            device_id=cross_peer, device_id_type=MESH,
        )

    def step_copy(p):
        return pltpu.make_async_remote_copy(
            src_ref=step_out.at[p], dst_ref=step_in.at[p],
            send_sem=step_send.at[p], recv_sem=step_recv.at[p],
            device_id=cross_peer, device_id_type=MESH,
        )

    for p in range(2):
        for i in range(4):
            if p == 1:
                for side, cond, gone in ((0, has_lo, has_hi), (1, has_hi, has_lo)):
                    @pl.when(cond)
                    def _(i=i, side=side):
                        halo_copy(i, side).wait_recv()
            derive(i, p)
            accumulate(i, p)
            if p == 0 and i == 0:
                for d in range(3):
                    gram_copy(d).start()
            if i % 2 == 0:
                mate_copy(i // 2, p).start()
            if i == 1:
                mate_copy(0, p).wait_recv()

                def add(t, carry, p=p):
                    for j in range(3):
                        total = sums[1, p, j, t] + mate[0, p, j, t]
                        top = jnp.maximum(jnp.max(jnp.abs(total), axis=(0, 1))[None], 1e-32)
                        step = (top * ((1.0 + 2.0**-7) / TOP)).astype(jnp.bfloat16).astype(jnp.float32)
                        code = jnp.round(total * (1.0 / step)[None]).astype(jnp.int32)
                        cross_out[p, j, t] = code.astype(jnp.int16).reshape(4, NY, LANES)
                        steps[j, pl.ds(t, 1)] = step
                    return carry

                lax.fori_loop(0, 12, add, 0)
                step_out[p] = steps[...].astype(jnp.bfloat16)
                step_copy(p).start()
                cross_copy(p).start()

    for d in range(3):
        gram_copy(d).wait()
    g = [gram_out[n] + gram_in[0, n] + gram_in[1, n] + gram_in[2, n] for n in range(5)]
    g00 = jnp.full((8, LANES), 4.0 * NS, jnp.float32)
    g01, g02, g11, g12, g22 = g
    c00 = g11 * g22 - g12 * g12
    c01 = g02 * g12 - g01 * g22
    c02 = g01 * g12 - g02 * g11
    c11 = g00 * g22 - g02 * g02
    c12 = g02 * g01 - g00 * g12
    c22 = g00 * g11 - g01 * g01
    det = g00 * c00 + g01 * c01 + g02 * c02
    inverse = [[x / det for x in row] for row in ((c00, c01, c02), (c01, c11, c12), (c02, c12, c22))]

    for p in range(2):
        mate_copy(1, p).wait_recv()
        step_copy(p).wait_recv()
        steps[...] = step_in[p].astype(jnp.float32)
        cross_copy(p).wait_recv()

        def solve(t, carry, p=p):
            total = [
                sums[3, p, j, t]
                + mate[1, p, j, t]
                + cross_in[p, j, t].astype(jnp.int32).astype(jnp.float32).reshape(8, 8, LANES)
                * steps[j, pl.ds(t, 1)][None]
                for j in range(3)
            ]
            for n in range(3):
                fit = sum(inverse[n][j][None] * total[j] for j in range(3)).reshape(4, NY, LANES)
                if p == 0:
                    out[n, t // 4, t % 4, 2:6] = fit
                else:
                    out[n, t // 4, t % 4, 0:2] = fit[:2]
                    out[n, t // 4, t % 4, 6:8] = fit[2:]
            return carry

        lax.fori_loop(0, 12, solve, 0)

    for i in range(4):
        for side, cond in ((0, has_hi), (1, has_lo)):
            @pl.when(cond)
            def _(i=i, side=side):
                halo_copy(i, side).wait_send()
    for p in range(2):
        cross_copy(p).wait_send()
        step_copy(p).wait_send()
        for half in range(2):
            mate_copy(half, p).wait_send()


def local(velocity, phase_bins):
    hbm = pl.BlockSpec(memory_space=pltpu.HBM)
    f32, bf16, dma = jnp.float32, jnp.bfloat16, pltpu.SemaphoreType.DMA
    block = (3, 12, 8, 8, LANES)
    return pl.pallas_call(
        kernel,
        out_shape=pltpu.VMEM((3, 3, 4, NP, NY, LANES), f32),
        in_specs=[hbm] * 2,
        out_specs=pl.BlockSpec(memory_space=pltpu.VMEM),
        scratch_shapes=[pltpu.VMEM(c, bf16) for c in ((2, 128, 128), (2, 64, 256), (64, 64), (NZ, NZ))]
        + [
            pltpu.SMEM((NS,), jnp.int32),
            pltpu.VMEM((NS, 3, NP, NY, NZ), bf16),
            pltpu.VMEM((4, NS, 2, 2, 2, NY, LANES), bf16),
            pltpu.VMEM((NS, 3, 8, 8, LANES), f32),
            pltpu.VMEM((2, NS, 8, LANES), f32),
            pltpu.VMEM((4, 2) + block, f32),
            pltpu.VMEM((2, 2) + block, f32),
            pltpu.VMEM((2, 3, 12, 4, NY, LANES), jnp.int16),
            pltpu.VMEM((2, 3, 12, 4, NY, LANES), jnp.int16),
            pltpu.VMEM((3, 16, LANES), f32),
            pltpu.VMEM((2, 3, 16, LANES), bf16),
            pltpu.VMEM((2, 3, 16, LANES), bf16),
            pltpu.VMEM((5, 8, LANES), f32),
            pltpu.VMEM((3, 5, 8, LANES), f32),
            dma, dma((4, 2)), dma((4, 2)), dma((2, 2)), dma((2, 2)), dma((2,)), dma((2,)), dma((2,)), dma((2,)), dma((3,)), dma((3,)), dma,
        ],
        compiler_params=pltpu.CompilerParams(collective_id=0, has_side_effects=True),
    )(velocity, phase_bins)


def solution(mesh):
    in_specs = (P("snap", None, "slab", None, None), P("snap"))
    out_specs = P(None, None, None, "slab", None, "snap")
    return jax.shard_map(local, mesh=mesh, in_specs=in_specs, out_specs=out_specs, check_vma=False)
```
